32 devices in a mesh: wide: 16 (over z, y, core), narrow: 2 (over x).
Axes of the slice: x: 2, y: 2, z: 4, core: 2. Of those that a mesh axis runs over, the one named last changes fastest.
Arguments:
- users: float32 [49152, 256], P(('wide', 'narrow')), may hold values from -1.5 to 1.5
- user_state: float32 [49152], P(('wide', 'narrow')), may hold values from 0.05 to 0.5
- items: float32 [8192, 256], P('wide'), may hold values from -1.5 to 1.5
- item_state: float32 [8192], P('wide'), may hold values from 0.05 to 0.5
- tile_ids: int32 [16, 2, 2, 16], P('wide', 'narrow'), may hold values from 0 to 47, as said below
- tile_count: int32 [16, 2, 2], P('wide', 'narrow'), may hold values from 1 to 16, as said below
- pos_items: int32 [16, 2, 2, 16, 128], P('wide', 'narrow'), may hold values from 0 to 127
- neg_offsets: int32 [16, 2, 2, 16], P('wide', 'narrow'), may hold values from 0 to 384
Outputs:
- new_users: float32 [49152, 256], P(('wide', 'narrow'))
- new_user_state: float32 [49152], P(('wide', 'narrow'))
- new_items: float32 [8192, 256], P('wide')
- new_item_state: float32 [8192], P('wide')
The draws below stay inside these ranges and needn't reach their ends.
Inputs may be any that keep to these rules, and one draw needn't show every extreme that they name: `tile_ids`: within one list the 16 ids are distinct tile numbers; slots at or after the count are ignored. `tile_count`: some entry equals 16.
All inputs are finite; a program needn't handle non-finite values.
Results may differ from the reference program's by a relative error of at most 0.0003.
Values sent between devices are 32-bit elements; how exact they have to be, the bound alone decides.
A program may use at most 64 MiB of HBM per device.

```python
import math
import jax
import jax.numpy as jnp
from jax import lax

K = 256
TILE = 128
U_DEV = 1536
ITEM_BLK = 512
TILES = 16
GROUP = 8
STRATA = 2
USERS = 49152
ITEMS = 8192
N_WIDE = 16
N_NARROW = 2


def draw_tile_ids(key, part):
    total = U_DEV // TILE * (ITEM_BLK // TILE)
    lists = N_WIDE * N_NARROW * STRATA
    keys = jax.random.split(jax.random.fold_in(key, 11), lists)
    chosen = jax.vmap(lambda single: jax.random.permutation(single, total)[:TILES])(keys)
    return chosen.reshape(N_WIDE, N_NARROW, STRATA, TILES).astype(jnp.int32)


def draw_tile_count(key, part):
    first = jax.random.randint(jax.random.fold_in(key, 21), (N_WIDE * N_NARROW * STRATA,), 0, TILES)
    second = jax.random.randint(jax.random.fold_in(key, 22), (N_WIDE * N_NARROW * STRATA,), 0, TILES)
    counts = 1 + first * second // TILES
    place = jax.random.randint(jax.random.fold_in(key, 23), (), 0, N_WIDE * N_NARROW * STRATA)
    counts = counts.at[place].set(TILES)
    return counts.reshape(N_WIDE, N_NARROW, STRATA).astype(jnp.int32)


def plant(drawn, key, low, largest):
    longest = drawn.shape.index(max(drawn.shape))
    spots = []
    for shift in (0, 1):
        where = [jax.random.randint(jax.random.fold_in(key, axis), (), 0, length) for axis, length in enumerate(drawn.shape)]
        where[longest] = (where[longest] + shift) % drawn.shape[longest]
        spots.append(tuple(where))
    return drawn.at[spots[0]].set(low).at[spots[1]].set(largest)


def levels(key, shape, cuts, low, top_value):
    def one(axis_at, shards_of):
        heights = jax.random.uniform(jax.random.fold_in(jax.random.fold_in(key, 6), axis_at), (shards_of,), jnp.float32, low / len(cuts), top_value / len(cuts))
        return jnp.repeat(jnp.exp(heights), shape[axis_at] // shards_of).reshape((-1,) + (1,) * (len(shape) - axis_at - 1))

    level = one(*cuts[0])
    for cut in cuts[1:]:
        level = level * one(*cut)
    return level


def noise(key, dims, spread, limit, pieces=(), held_as=jnp.bfloat16):
    drawn = jax.random.normal(key, dims, jnp.float32) * spread
    if len(pieces) > 0:
        drawn = levels(key, dims, pieces, -0.22, 0.18) * drawn
    return jnp.clip(drawn, min=-limit, max=limit).astype(held_as)


def setup_inputs(seed: int = 0) -> dict:
    splits = jax.random.split(jax.random.key(seed), 9)
    users = noise(splits[0], (USERS, K), 0.25, 1.5, ((0, 32),), jnp.float32)
    user_state = jnp.clip(jnp.exp(math.log(0.5) - 2.3025851 * jax.random.uniform(splits[1], (USERS,), jnp.float32) ** levels(splits[1], (USERS,), ((0, 32),), -0.2, 0.2)), 0.05, 0.5)
    items = noise(splits[2], (ITEMS, K), 0.25, 1.5, ((0, 16),), jnp.float32)
    item_state = jnp.clip(jnp.exp(math.log(0.5) - 2.3025851 * jax.random.uniform(splits[3], (ITEMS,), jnp.float32) ** levels(splits[3], (ITEMS,), ((0, 16),), -0.2, 0.2)), 0.05, 0.5)
    tile_ids = draw_tile_ids(jax.random.fold_in(splits[8], 71), 0)
    tile_count = draw_tile_count(jax.random.fold_in(splits[8], 71), 0)
    pos_items = plant(jax.random.randint(splits[6], (N_WIDE, N_NARROW, STRATA, TILES, TILE), 0, TILE), jax.random.fold_in(splits[6], 1), 0, TILE - 1).astype(jnp.int32)
    neg_offsets = plant(jax.random.randint(splits[7], (N_WIDE, N_NARROW, STRATA, TILES), 0, ITEM_BLK - TILE + 1), jax.random.fold_in(splits[7], 1), 0, ITEM_BLK - TILE).astype(jnp.int32)
    return {"users": users, "user_state": user_state, "items": items, "item_state": item_state, "tile_ids": tile_ids, "tile_count": tile_count, "pos_items": pos_items, "neg_offsets": neg_offsets}


highest = lax.Precision.HIGHEST
step_rate = 0.25

def adagrad(values, state, grad):
    new_state = state + lax.optimization_barrier(jnp.mean(grad * grad, axis=-1))
    return (values - step_rate * grad / jnp.sqrt(new_state)[..., None], new_state)

def group_update(carry, user_tiles, block_tiles, negatives, tile_list, positives, offsets, live):
    user_grad, pos_grad, neg_grad = carry
    row_count = user_tiles.shape[0]
    col_count = block_tiles.shape[0]
    side = user_tiles.shape[1]
    width = user_tiles.shape[2]
    lanes = jnp.arange(side, dtype=jnp.int32)
    row_index = (tile_list // col_count).astype(jnp.int32)
    col_index = (tile_list % col_count).astype(jnp.int32)
    factors = user_tiles[row_index]
    column_block = block_tiles[col_index]
    onehot = (positives[:, :, None] == lanes[None, None, :]).astype(jnp.float32)
    pos_rows = jnp.einsum('gui,gik->guk', onehot, column_block, precision=highest)
    neg_rows = jax.vmap(lambda start: lax.dynamic_slice_in_dim(negatives, start, side, 0))(offsets)
    pos_score = lax.optimization_barrier(jnp.sum(factors * pos_rows, axis=-1))
    neg_score = jnp.einsum('guk,gjk->guj', factors, neg_rows, precision=highest)
    coeffs = jax.nn.sigmoid(neg_score - pos_score[:, :, None]) * (live[:, None, None] / side)
    totals = lax.optimization_barrier(jnp.sum(coeffs, axis=-1))
    factor_grad = jnp.einsum('guj,gjk->guk', coeffs, neg_rows, precision=highest) - totals[:, :, None] * pos_rows
    positive_grad = -jnp.einsum('gui,guk->gik', onehot, totals[:, :, None] * factors, precision=highest)
    negative_grad = jnp.einsum('guj,guk->gjk', coeffs, factors, precision=highest)
    row_hot = (row_index[:, None] == jnp.arange(row_count, dtype=jnp.int32)[None, :]).astype(jnp.float32)
    col_hot = (col_index[:, None] == jnp.arange(col_count, dtype=jnp.int32)[None, :]).astype(jnp.float32)
    user_grad = user_grad + jnp.einsum('gr,guk->ruk', row_hot, factor_grad, precision=highest)
    pos_grad = pos_grad + jnp.einsum('gc,gik->cik', col_hot, positive_grad, precision=highest)
    neg_index = (offsets[:, None] + lanes[None, :]).reshape(-1)
    neg_grad = neg_grad.at[neg_index].add(negative_grad.reshape(-1, width))
    return (user_grad, pos_grad, neg_grad)

def device_grads(users, block, negatives, tile_list, count, positives, offsets):
    width = users.shape[1]
    user_tiles = users.reshape(-1, TILE, width)
    block_tiles = block.reshape(-1, TILE, width)
    groups = tile_list.shape[0] // GROUP
    slots = jnp.arange(tile_list.shape[0], dtype=jnp.int32)
    live = (slots < count).astype(jnp.float32)
    init = (jnp.zeros(user_tiles.shape, jnp.float32), jnp.zeros(block_tiles.shape, jnp.float32), jnp.zeros(block.shape, jnp.float32))

    def advance(carry, inputs):
        return (group_update(carry, user_tiles, block_tiles, negatives, inputs[0], inputs[1], inputs[2], inputs[3]), None)
    inputs = (tile_list.reshape(groups, GROUP), positives.reshape(groups, GROUP, TILE), offsets.reshape(groups, GROUP), live.reshape(groups, GROUP))
    carry, unused = lax.scan(advance, init, inputs)
    return (carry[0].reshape(users.shape), carry[1].reshape(block.shape), carry[2])

def reference(users, user_state, items, item_state, tile_ids, tile_count, pos_items, neg_offsets):
    wide_count = N_WIDE
    users_r = users.reshape(wide_count, N_NARROW, U_DEV, K)
    state_r = user_state.reshape(wide_count, N_NARROW, U_DEV)
    blocks = items.reshape(wide_count, ITEM_BLK, K)
    block_state = item_state.reshape(wide_count, ITEM_BLK)
    for stratum in range(STRATA):
        current = jnp.roll(blocks, stratum, 0)
        opposite = jnp.roll(current, wide_count // 2, 0)

        def one_position(index, current=current, opposite=opposite, users_r=users_r, state_r=state_r, stratum=stratum):
            grads = jax.vmap(device_grads, in_axes=(0, None, None, 0, 0, 0, 0))(users_r[index], current[index], opposite[index], tile_ids[index, :, stratum], tile_count[index, :, stratum], pos_items[index, :, stratum], neg_offsets[index, :, stratum])
            fresh_users, fresh_state = adagrad(users_r[index], state_r[index], grads[0])
            return (fresh_users, fresh_state, lax.optimization_barrier(jnp.sum(grads[1], axis=0)), lax.optimization_barrier(jnp.sum(grads[2], axis=0)))
        users_r, state_r, pos_sum, neg_sum = lax.map(one_position, jnp.arange(wide_count, dtype=jnp.int32))
        total = pos_sum + jnp.roll(neg_sum, wide_count // 2, 0)
        by_block = jnp.roll(total, -stratum, 0)
        blocks, block_state = adagrad(blocks, block_state, by_block)
    return (users_r.reshape(-1, K), state_r.reshape(-1), blocks.reshape(-1, K), block_state.reshape(-1))
```

```python
import functools

import jax
import jax.numpy as jnp
from jax import lax
from jax.experimental import pallas as pl
from jax.experimental.pallas import tpu as pltpu
from jax.sharding import PartitionSpec as P

TILE = 128
STRATA = 2
BATCH = 4
CHUNKS = 4
WINDOW = TILE + 16
MESH = pl.DeviceIdType.MESH
step_rate = 0.25
f32 = jnp.float32
bf16 = jnp.bfloat16
VMEM = pltpu.MemorySpace.VMEM
SMEM = pltpu.MemorySpace.SMEM


def dot(a, b, dims):
    return lax.dot_general(a, b, (dims, ((), ())), preferred_element_type=f32)


def pair(x):
    high = x.astype(bf16)
    low = (x - high.astype(f32)).astype(bf16)
    return jnp.concatenate([high, low], axis=0)


def tiles_kernel(
    stratum, ids, count, offsets, positives, users, state, block, negatives,
    new_users, new_state, pos_grad, neg_grad, split, square, padded, spread,
):
    cols = block.shape[0] // TILE
    rows = users.shape[0] // TILE
    side = TILE
    width = users.shape[1]
    new_users[...] = jnp.zeros(new_users.shape, f32)
    pos_grad[...] = jnp.zeros(pos_grad.shape, f32)
    spread[...] = jnp.zeros(spread.shape, f32)
    length = negatives.shape[0]
    padded[0:length, :] = negatives[...]
    padded[length:, :] = jnp.zeros((padded.shape[0] - length, width), f32)
    for col in range(cols):
        split[col] = pair(block[col * side : (col + 1) * side, :])
    live_count = count[stratum]
    item = lax.broadcasted_iota(jnp.int32, (side, side), 0)
    place = lax.broadcasted_iota(jnp.int32, (side, WINDOW), 1)

    def batch(step, carry):
        work = []
        for lane in range(BATCH):
            slot = step * BATCH + lane
            tile = ids[stratum, slot]
            within = lax.rem(offsets[stratum, slot], 8)
            window = pl.ds(pl.multiple_of(offsets[stratum, slot] - within, 8), WINDOW)
            row = pl.multiple_of(lax.div(tile, cols) * side, side)
            col = lax.rem(tile, cols)
            live = jnp.where(slot < live_count, 1.0 / side, 0.0).astype(f32)
            factors = users[pl.ds(row, side), :]
            factors_low = factors.astype(bf16)
            neg_rows = padded[window, :].astype(bf16)
            hot = jnp.where(item == positives[stratum, pl.ds(slot, 1), :], 1.0, 0.0).astype(f32)
            hot_t = hot.T.astype(bf16)
            hot = hot.astype(bf16)
            pos_rows = dot(jnp.concatenate([hot_t, hot_t], axis=1), split[col], ((1,), (0,)))
            neg_score = dot(factors_low, neg_rows, ((1,), (1,)))
            pos_score = jnp.sum(factors * pos_rows, axis=-1, keepdims=True)
            chosen = jnp.logical_and(place >= within, place < within + side)
            coeffs = jnp.where(chosen, live, 0.0) / (1.0 + jnp.exp(pos_score - neg_score))
            totals = jnp.sum(coeffs, axis=-1, keepdims=True)
            coeffs_low = coeffs.astype(bf16)
            factor_grad = dot(coeffs_low, neg_rows, ((1,), (0,))) - totals * pos_rows
            positive = dot(
                jnp.concatenate([hot, hot], axis=1), pair(totals * factors), ((1,), (0,))
            )
            negative = dot(coeffs.T.astype(bf16), factors_low, ((1,), (0,)))
            work.append((row, col, window, factor_grad, positive, negative))
        for row, col, window, factor_grad, positive, negative in work:
            new_users[pl.ds(row, side), :] += factor_grad
            at = pl.ds(pl.multiple_of(col * side, side), side)
            pos_grad[at, :] -= positive
            spread[window, :] += negative
        return carry

    lax.fori_loop(0, lax.div(live_count + (BATCH - 1), BATCH), batch, 0)
    neg_grad[...] = spread[0:length, :]
    square[...] = jnp.zeros(square.shape, f32)
    square[0:rows, :] = state[...]
    sums = square[...].T
    for row in range(rows):
        at = slice(row * side, (row + 1) * side)
        grad = new_users[at, :]
        fresh = sums[:, row : row + 1] + jnp.sum(grad * grad, axis=-1, keepdims=True) * (1.0 / width)
        new_users[at, :] = users[at, :] - (step_rate / jnp.sqrt(fresh)) * grad
        square[:, row : row + 1] = fresh
    new_state[...] = square[...].T[0:rows, :]


def run_tiles(stratum, ids, count, offsets, positives, users, state, block, negatives):
    width = users.shape[1]
    cols = block.shape[0] // TILE
    return pl.pallas_call(
        functools.partial(tiles_kernel, stratum),
        out_shape=(
            jax.ShapeDtypeStruct(users.shape, f32),
            jax.ShapeDtypeStruct(state.shape, f32),
            jax.ShapeDtypeStruct(block.shape, f32),
            jax.ShapeDtypeStruct(block.shape, f32),
        ),
        in_specs=[pl.BlockSpec(memory_space=SMEM)] * 3 + [pl.BlockSpec(memory_space=VMEM)] * 5,
        out_specs=(pl.BlockSpec(memory_space=VMEM),) * 4,
        scratch_shapes=[
            pltpu.VMEM((cols, 2 * TILE, width), bf16),
            pltpu.VMEM((TILE, TILE), f32),
            pltpu.VMEM((block.shape[0] + 16, width), f32),
            pltpu.VMEM((block.shape[0] + 16, width), f32),
        ],
        compiler_params=pltpu.CompilerParams(vmem_limit_bytes=40 * 1024 * 1024),
        name="tiles",
    )(ids, count, offsets, positives, users, state, block, negatives)


def greet(devices):
    barrier = pltpu.get_barrier_semaphore()
    for device in devices:
        pl.semaphore_signal(barrier, inc=1, device_id=device, device_id_type=MESH)
    pl.semaphore_wait(barrier, len(devices))


def send(src, dst, sems, kind, chunk, device):
    copy = pltpu.make_async_remote_copy(
        src_ref=src,
        dst_ref=dst,
        send_sem=sems.at[0, kind, chunk],
        recv_sem=sems.at[1, kind, chunk],
        device_id=device,
        device_id_type=MESH,
    )
    copy.start()
    return copy


def fetch_kernel(wide, block, negatives, sems):
    w, r = lax.axis_index("wide"), lax.axis_index("narrow")
    across = (lax.rem(w + wide // 2, wide), r)
    beside = (w, 1 - r)
    greet([across, beside])
    half = block.shape[0] // 2
    size = half // CHUNKS
    far, near = [], []

    def part(chunk):
        return pl.ds(pl.multiple_of(r * half + chunk * size, size), size)

    for c in range(CHUNKS):
        far.append(send(block.at[part(c), :], negatives.at[part(c), :], sems, 0, c, across))
    for c in range(CHUNKS):
        far[c].wait_recv()
        near.append(send(negatives.at[part(c), :], negatives.at[part(c), :], sems, 1, c, beside))
    for c in range(CHUNKS):
        far[c].wait_send()
        near[c].wait()


def run_fetch(block):
    return pl.pallas_call(
        functools.partial(fetch_kernel, lax.axis_size("wide")),
        out_shape=jax.ShapeDtypeStruct(block.shape, f32),
        in_specs=[pl.BlockSpec(memory_space=VMEM)],
        out_specs=pl.BlockSpec(memory_space=VMEM),
        scratch_shapes=[pltpu.SemaphoreType.DMA((2, 2, CHUNKS))],
        compiler_params=pltpu.CompilerParams(collective_id=0, has_side_effects=True),
        name="fetch",
    )(block)


def exchange_kernel(wide, shifts, last, *refs):
    pos_grad, neg_grad, block, state = refs[:4]
    outs = refs[4 : 4 + len(shifts)]
    new_state = refs[4 + len(shifts)]
    beside_neg, beside_pos, across_neg, summed, fresh_half, fresh_state, square, sems = refs[
        5 + len(shifts) :
    ]
    w, r = lax.axis_index("wide"), lax.axis_index("narrow")
    across = (lax.rem(w + wide // 2, wide), r)
    beside = (w, 1 - r)
    targets = [(lax.rem(w + shift + wide, wide), r) for shift in shifts]
    sources = [(lax.rem(w - shift + wide, wide), r) for shift in shifts]
    greet([beside, across] + targets + sources)
    width = block.shape[1]
    half = block.shape[0] // 2
    size = half // CHUNKS
    side = TILE

    def part(which, chunk):
        return pl.ds(pl.multiple_of(which * half + chunk * size, size), size)

    def local(chunk):
        return slice(chunk * size, (chunk + 1) * size)

    side_neg = [
        send(neg_grad.at[part(1 - r, c), :], beside_neg.at[local(c), :], sems, 0, c, beside)
        for c in range(CHUNKS)
    ]
    side_pos = [
        send(pos_grad.at[part(1 - r, c), :], beside_pos.at[local(c), :], sems, 1, c, beside)
        for c in range(CHUNKS)
    ]
    square[...] = jnp.zeros(square.shape, f32)
    square[0 : half // side, :] = state[r]
    sums = square[...].T
    far = []
    for c in range(CHUNKS):
        side_neg[c].wait_recv()
        summed[local(c), :] = neg_grad[part(r, c), :] + beside_neg[local(c), :]
        far.append(send(summed.at[local(c), :], across_neg.at[local(c), :], sems, 2, c, across))
    moved = [[] for shift in shifts]
    for c in range(CHUNKS):
        side_pos[c].wait_recv()
        far[c].wait_recv()
        grad = pos_grad[part(r, c), :] + beside_pos[local(c), :] + across_neg[local(c), :]
        row, begin = c * size // side, c * size % side
        fresh = sums[begin : begin + size, row : row + 1] + jnp.sum(
            grad * grad, axis=-1, keepdims=True
        ) * (1.0 / width)
        fresh_half[local(c), :] = block[part(r, c), :] - (step_rate / jnp.sqrt(fresh)) * grad
        square[begin : begin + size, row : row + 1] = fresh
        for k in reversed(range(len(shifts))):
            moved[k].append(
                send(
                    fresh_half.at[local(c), :], outs[k].at[part(r, c), :], sems, 3 + k, c, targets[k]
                )
            )
    fresh_state[...] = square[...].T[0 : half // side, :]
    state_moved = send(fresh_state, new_state.at[r], sems, 7, 0, targets[0])
    relayed = []
    for c in range(CHUNKS):
        for k in range(len(shifts)):
            moved[k][c].wait_recv()
            relayed.append(
                send(outs[k].at[part(r, c), :], outs[k].at[part(r, c), :], sems, 5 + k, c, beside)
            )
    state_moved.wait_recv()
    if last:
        relayed.append(send(new_state.at[r], new_state.at[r], sems, 7, 1, beside))
    for copies in [side_neg, side_pos, far] + moved + [[state_moved]]:
        for copy in copies:
            copy.wait_send()
    for copy in relayed:
        copy.wait()


def run_exchange(shifts, last, pos_grad, neg_grad, block, state):
    half = (block.shape[0] // 2, block.shape[1])
    outs = (jax.ShapeDtypeStruct(block.shape, f32),) * len(shifts)
    return pl.pallas_call(
        functools.partial(exchange_kernel, lax.axis_size("wide"), shifts, last),
        out_shape=outs + (jax.ShapeDtypeStruct(state.shape, f32),),
        in_specs=[pl.BlockSpec(memory_space=VMEM)] * 4,
        out_specs=(pl.BlockSpec(memory_space=VMEM),) * (len(shifts) + 1),
        scratch_shapes=[pltpu.VMEM(half, f32)] * 5
        + [
            pltpu.VMEM(state.shape[1:], f32),
            pltpu.VMEM((TILE, TILE), f32),
            pltpu.SemaphoreType.DMA((2, 8, CHUNKS)),
        ],
        compiler_params=pltpu.CompilerParams(
            collective_id=2 if last else 1,
            has_side_effects=True,
            vmem_limit_bytes=24 * 1024 * 1024,
        ),
        name="exchange",
    )(pos_grad, neg_grad, block, state)


def passed_along(block, distance):
    size = lax.axis_size("wide")
    return lax.ppermute(block, "wide", [((i - distance) % size, i) for i in range(size)])


def general_exchange(shift, pos_grad, neg_grad, block, state):
    half = lax.axis_size("wide") // 2
    total = lax.psum(pos_grad + passed_along(neg_grad, half), "narrow")
    new_state = state + jnp.mean(total * total, axis=-1)
    block = block - step_rate * total / jnp.sqrt(new_state)[:, None]
    return passed_along((block, new_state), shift)


def per_device(users, user_state, items, item_state, tile_ids, tile_count, pos_items, neg_offsets):
    wide, narrow = lax.axis_size("wide"), lax.axis_size("narrow")
    ids, count = tile_ids[0, 0], tile_count[0, 0]
    positives, offsets = pos_items[0, 0], neg_offsets[0, 0]
    own_state = user_state.reshape(-1, TILE)
    block, block_state = items, item_state
    paired = narrow == 2
    if paired:
        block_state = item_state.reshape(2, -1, TILE)
        negatives = run_fetch(block)
    else:
        negatives = passed_along(block, wide // 2)
    for stratum in range(STRATA):
        users, own_state, pos_grad, neg_grad = run_tiles(
            stratum, ids, count, offsets, positives, users, own_state, block, negatives
        )
        last = stratum + 1 == STRATA
        if paired:
            shifts = (1 - STRATA,) if last else (1, 1 + wide // 2)
            results = run_exchange(shifts, last, pos_grad, neg_grad, block, block_state)
            block, block_state = results[0], results[-1]
            negatives = results[1]
        else:
            block, block_state = general_exchange(
                1 - STRATA if last else 1, pos_grad, neg_grad, block, block_state
            )
            if not last:
                negatives = passed_along(block, wide // 2)
    return (users, own_state.reshape(user_state.shape), block, block_state.reshape(item_state.shape))


def solution(mesh):
    return jax.shard_map(
        per_device,
        mesh=mesh,
        in_specs=(
            P(("wide", "narrow"), None),
            P(("wide", "narrow")),
            P("wide", None),
            P("wide"),
            P("wide", "narrow", None, None),
            P("wide", "narrow", None),
            P("wide", "narrow", None, None, None),
            P("wide", "narrow", None, None),
        ),
        out_specs=(P(("wide", "narrow"), None), P(("wide", "narrow")), P("wide", None), P("wide")),
        check_vma=False,
    )
```

```python
import functools

import jax
import jax.numpy as jnp
from jax import lax
from jax.experimental import pallas as pl
from jax.experimental.pallas import tpu as pltpu
from jax.sharding import PartitionSpec as P

TILE = 128
STRATA = 2
BATCH = 4
CHUNKS = 8
AHEAD = 8
LAG_FRESH = 4
LAG_RELAY = 6
WINDOW = TILE + 16
MESH = pl.DeviceIdType.MESH
step_rate = 0.25
f32 = jnp.float32
bf16 = jnp.bfloat16
VMEM = pltpu.MemorySpace.VMEM
SMEM = pltpu.MemorySpace.SMEM


def dot(a, b, dims):
    return lax.dot_general(a, b, (dims, ((), ())), preferred_element_type=f32)


def pair(x):
    high = x.astype(bf16)
    low = (x - high.astype(f32)).astype(bf16)
    return jnp.concatenate([high, low], axis=0)


def tiles_kernel(
    stratum, ids, count, offsets, positives, users, state, block, negatives,
    new_users, new_state, pos_grad, neg_grad, split, square, padded, spread,
):
    cols = block.shape[0] // TILE
    rows = users.shape[0] // TILE
    side = TILE
    width = users.shape[1]
    new_users[...] = jnp.zeros(new_users.shape, f32)
    pos_grad[...] = jnp.zeros(pos_grad.shape, f32)
    spread[...] = jnp.zeros(spread.shape, f32)
    length = negatives.shape[0]
    padded[0:length, :] = negatives[...]
    padded[length:, :] = jnp.zeros((padded.shape[0] - length, width), f32)
    for col in range(cols):
        split[col] = pair(block[col * side : (col + 1) * side, :])
    live_count = count[0, stratum]
    item = lax.broadcasted_iota(jnp.int32, (side, side), 0)
    place = lax.broadcasted_iota(jnp.int32, (side, WINDOW), 1)

    def batch(step, carry):
        work = []
        for lane in range(BATCH):
            slot = step * BATCH + lane
            tile = ids[stratum, slot]
            within = lax.rem(offsets[stratum, slot], 8)
            window = pl.ds(pl.multiple_of(offsets[stratum, slot] - within, 8), WINDOW)
            row = pl.multiple_of(lax.div(tile, cols) * side, side)
            col = lax.rem(tile, cols)
            live = jnp.where(slot < live_count, 1.0 / side, 0.0).astype(f32)
            factors = users[pl.ds(row, side), :]
            factors_low = factors.astype(bf16)
            neg_rows = padded[window, :].astype(bf16)
            hot = jnp.where(item == positives[stratum, pl.ds(slot, 1), :], 1.0, 0.0).astype(f32)
            hot_t = hot.T.astype(bf16)
            hot = hot.astype(bf16)
            pos_rows = dot(jnp.concatenate([hot_t, hot_t], axis=1), split[col], ((1,), (0,)))
            neg_score = dot(factors_low, neg_rows, ((1,), (1,)))
            pos_score = jnp.sum(factors * pos_rows, axis=-1, keepdims=True)
            chosen = jnp.logical_and(place >= within, place < within + side)
            coeffs = jnp.where(chosen, live, 0.0) / (1.0 + jnp.exp(pos_score - neg_score))
            totals = jnp.sum(coeffs, axis=-1, keepdims=True)
            coeffs_low = coeffs.astype(bf16)
            factor_grad = dot(coeffs_low, neg_rows, ((1,), (0,))) - totals * pos_rows
            positive = dot(
                jnp.concatenate([hot, hot], axis=1), pair(totals * factors), ((1,), (0,))
            )
            negative = dot(coeffs.T.astype(bf16), factors_low, ((1,), (0,)))
            work.append((row, col, window, factor_grad, positive, negative))
        for row, col, window, factor_grad, positive, negative in work:
            new_users[pl.ds(row, side), :] += factor_grad
            at = pl.ds(pl.multiple_of(col * side, side), side)
            pos_grad[at, :] -= positive
            spread[window, :] += negative
        return carry

    lax.fori_loop(0, lax.div(live_count + (BATCH - 1), BATCH), batch, 0)
    neg_grad[...] = spread[0:length, :]
    square[...] = jnp.zeros(square.shape, f32)
    square[0:rows, :] = state[...]
    sums = square[...].T
    for row in range(rows):
        at = slice(row * side, (row + 1) * side)
        grad = new_users[at, :]
        fresh = sums[:, row : row + 1] + jnp.sum(grad * grad, axis=-1, keepdims=True) * (1.0 / width)
        new_users[at, :] = users[at, :] - (step_rate / jnp.sqrt(fresh)) * grad
        square[:, row : row + 1] = fresh
    new_state[...] = square[...].T[0:rows, :]


def run_tiles(stratum, ids, count, offsets, positives, users, state, block, negatives):
    width = users.shape[1]
    cols = block.shape[0] // TILE
    return pl.pallas_call(
        functools.partial(tiles_kernel, stratum),
        out_shape=(
            jax.ShapeDtypeStruct(users.shape, f32),
            jax.ShapeDtypeStruct(state.shape, f32),
            jax.ShapeDtypeStruct(block.shape, f32),
            jax.ShapeDtypeStruct(block.shape, f32),
        ),
        in_specs=[pl.BlockSpec(memory_space=SMEM)] * 3 + [pl.BlockSpec(memory_space=VMEM)] * 5,
        out_specs=(pl.BlockSpec(memory_space=VMEM),) * 4,
        scratch_shapes=[
            pltpu.VMEM((cols, 2 * TILE, width), bf16),
            pltpu.VMEM((TILE, TILE), f32),
            pltpu.VMEM((block.shape[0] + 16, width), f32),
            pltpu.VMEM((block.shape[0] + 16, width), f32),
        ],
        compiler_params=pltpu.CompilerParams(vmem_limit_bytes=24 * 1024 * 1024),
        name="tiles",
    )(ids, count, offsets, positives, users, state, block, negatives)


def greet(devices):
    barrier = pltpu.get_barrier_semaphore()
    for device in devices:
        pl.semaphore_signal(barrier, inc=1, device_id=device, device_id_type=MESH)
    pl.semaphore_wait(barrier, len(devices))


def send(src, dst, sems, kind, chunk, device):
    copy = pltpu.make_async_remote_copy(
        src_ref=src,
        dst_ref=dst,
        send_sem=sems.at[0, kind, chunk],
        recv_sem=sems.at[1, kind, chunk],
        device_id=device,
        device_id_type=MESH,
    )
    copy.start()
    return copy


def fetch_kernel(wide, count, *refs):
    block, negatives = refs[0], refs[count]
    sems, local_sems = refs[2 * count + 1 :]
    w, r = lax.axis_index("wide"), lax.axis_index("narrow")
    across = (lax.rem(w + wide // 2, wide), r)
    beside = (w, 1 - r)
    greet([across, beside])
    copies = []
    half = block.shape[0] // 2
    size = half // CHUNKS
    far, near = [], []

    def part(chunk):
        return pl.ds(pl.multiple_of(r * half + chunk * size, size), size)

    for c in range(CHUNKS):
        far.append(send(block.at[part(c), :], negatives.at[part(c), :], sems, 0, c, across))
    for k in range(count):
        copies.append(pltpu.make_async_copy(refs[k], refs[count + 1 + k], local_sems.at[k]))
        copies[k].start()
    for c in range(CHUNKS):
        far[c].wait_recv()
        near.append(send(negatives.at[part(c), :], negatives.at[part(c), :], sems, 1, c, beside))
    for c in range(CHUNKS):
        far[c].wait_send()
        near[c].wait()
    for copy in copies:
        copy.wait()


def run_fetch(*arrays):
    count = len(arrays)
    shapes = [jax.ShapeDtypeStruct(array.shape, array.dtype) for array in (arrays[0],) + arrays]
    return pl.pallas_call(
        functools.partial(fetch_kernel, lax.axis_size("wide"), count),
        out_shape=shapes,
        in_specs=[pl.BlockSpec(memory_space=pltpu.MemorySpace.HBM)] * count,
        out_specs=[pl.BlockSpec(memory_space=VMEM)] * (count + 1),
        scratch_shapes=[
            pltpu.SemaphoreType.DMA((2, 2, CHUNKS)),
            pltpu.SemaphoreType.DMA((count,)),
        ],
        compiler_params=pltpu.CompilerParams(
            collective_id=0, has_side_effects=True, vmem_limit_bytes=8 * 1024 * 1024
        ),
        name="fetch",
    )(*[pltpu.with_memory_space_constraint(a, pltpu.MemorySpace.HBM) for a in arrays])


def exchange_kernel(wide, shifts, last, *refs):
    pos_grad, neg_grad, block, state = refs[:4]
    outs = refs[4 : 4 + len(shifts)]
    new_state = refs[4 + len(shifts)]
    beside_neg, beside_pos, across_neg, summed, fresh_half, fresh_state, square, sems = refs[
        5 + len(shifts) :
    ]
    w, r = lax.axis_index("wide"), lax.axis_index("narrow")
    across = (lax.rem(w + wide // 2, wide), r)
    beside = (w, 1 - r)
    targets = [(lax.rem(w + shift + wide, wide), r) for shift in shifts]
    sources = [(lax.rem(w - shift + wide, wide), r) for shift in shifts]
    greet([beside, across] + targets + sources)
    width = block.shape[1]
    half = block.shape[0] // 2
    size = half // CHUNKS
    side = TILE

    def part(which, chunk):
        return pl.ds(pl.multiple_of(which * half + chunk * size, size), size)

    def local(chunk):
        return slice(chunk * size, (chunk + 1) * size)

    side_neg, side_pos, far, relayed = [], [], [], []
    moved = [[] for shift in shifts]

    def send_neg(c):
        side_neg.append(
            send(neg_grad.at[part(1 - r, c), :], beside_neg.at[local(c), :], sems, 0, c, beside)
        )

    def send_pos(c):
        side_pos.append(
            send(pos_grad.at[part(1 - r, c), :], beside_pos.at[local(c), :], sems, 1, c, beside)
        )

    def send_sum(c):
        side_neg[c].wait_recv()
        summed[local(c), :] = neg_grad[part(r, c), :] + beside_neg[local(c), :]
        far.append(send(summed.at[local(c), :], across_neg.at[local(c), :], sems, 2, c, across))

    def send_fresh(c):
        side_pos[c].wait_recv()
        far[c].wait_recv()
        grad = pos_grad[part(r, c), :] + beside_pos[local(c), :] + across_neg[local(c), :]
        row, begin = c * size // side, c * size % side
        fresh = sums[begin : begin + size, row : row + 1] + jnp.sum(
            grad * grad, axis=-1, keepdims=True
        ) * (1.0 / width)
        fresh_half[local(c), :] = block[part(r, c), :] - (step_rate / jnp.sqrt(fresh)) * grad
        square[begin : begin + size, row : row + 1] = fresh
        for k in reversed(range(len(shifts))):
            moved[k].append(
                send(
                    fresh_half.at[local(c), :], outs[k].at[part(r, c), :], sems, 3 + k, c, targets[k]
                )
            )

    def relay(c):
        for k in range(len(shifts)):
            moved[k][c].wait_recv()
            relayed.append(
                send(outs[k].at[part(r, c), :], outs[k].at[part(r, c), :], sems, 5 + k, c, beside)
            )

    for c in range(AHEAD):
        send_neg(c)
    square[...] = jnp.zeros(square.shape, f32)
    square[0 : half // side, :] = state[r]
    sums = square[...].T
    state_moved = None
    for step in range(CHUNKS + LAG_RELAY):
        if step < CHUNKS:
            send_sum(step)
            if step + AHEAD < CHUNKS:
                send_neg(step + AHEAD)
            send_pos(step)
        if 0 <= step - LAG_FRESH < CHUNKS:
            send_fresh(step - LAG_FRESH)
            if step - LAG_FRESH == CHUNKS - 1:
                fresh_state[...] = square[...].T[0 : half // side, :]
                state_moved = send(fresh_state, new_state.at[r], sems, 7, 0, targets[0])
        if 0 <= step - LAG_RELAY:
            relay(step - LAG_RELAY)
    state_moved.wait_recv()
    if last:
        relayed.append(send(new_state.at[r], new_state.at[r], sems, 7, 1, beside))
    for copies in [side_neg, side_pos, far] + moved + [[state_moved]]:
        for copy in copies:
            copy.wait_send()
    for copy in relayed:
        copy.wait()


def run_exchange(shifts, last, pos_grad, neg_grad, block, state):
    half = (block.shape[0] // 2, block.shape[1])
    outs = (jax.ShapeDtypeStruct(block.shape, f32),) * len(shifts)
    return pl.pallas_call(
        functools.partial(exchange_kernel, lax.axis_size("wide"), shifts, last),
        out_shape=outs + (jax.ShapeDtypeStruct(state.shape, f32),),
        in_specs=[pl.BlockSpec(memory_space=VMEM)] * 4,
        out_specs=(pl.BlockSpec(memory_space=VMEM),) * (len(shifts) + 1),
        scratch_shapes=[pltpu.VMEM(half, f32)] * 5
        + [
            pltpu.VMEM(state.shape[1:], f32),
            pltpu.VMEM((TILE, TILE), f32),
            pltpu.SemaphoreType.DMA((2, 8, CHUNKS)),
        ],
        compiler_params=pltpu.CompilerParams(
            collective_id=2 if last else 1,
            has_side_effects=True,
            vmem_limit_bytes=12 * 1024 * 1024,
        ),
        name="exchange",
    )(pos_grad, neg_grad, block, state)


def passed_along(block, distance):
    size = lax.axis_size("wide")
    return lax.ppermute(block, "wide", [((i - distance) % size, i) for i in range(size)])


def general_exchange(shift, pos_grad, neg_grad, block, state):
    half = lax.axis_size("wide") // 2
    total = lax.psum(pos_grad + passed_along(neg_grad, half), "narrow")
    new_state = state + jnp.mean(total * total, axis=-1)
    block = block - step_rate * total / jnp.sqrt(new_state)[:, None]
    return passed_along((block, new_state), shift)


def per_device(users, user_state, items, item_state, tile_ids, tile_count, pos_items, neg_offsets):
    wide, narrow = lax.axis_size("wide"), lax.axis_size("narrow")
    ids, count = tile_ids[0, 0], tile_count[0]
    positives, offsets = pos_items[0, 0], neg_offsets[0, 0]
    own_state = user_state.reshape(-1, TILE)
    block, block_state = items, item_state
    paired = narrow == 2
    if paired:
        block_state = item_state.reshape(2, -1, TILE)
        negatives, block, users, own_state, positives, block_state, ids, count, offsets = run_fetch(
            block, users, own_state, positives, block_state, ids, count, offsets
        )
    else:
        negatives = passed_along(block, wide // 2)
    for stratum in range(STRATA):
        users, own_state, pos_grad, neg_grad = run_tiles(
            stratum, ids, count, offsets, positives, users, own_state, block, negatives
        )
        last = stratum + 1 == STRATA
        if paired:
            shifts = (1 - STRATA,) if last else (1, 1 + wide // 2)
            results = run_exchange(shifts, last, pos_grad, neg_grad, block, block_state)
            block, block_state = results[0], results[-1]
            negatives = results[1]
        else:
            block, block_state = general_exchange(
                1 - STRATA if last else 1, pos_grad, neg_grad, block, block_state
            )
            if not last:
                negatives = passed_along(block, wide // 2)
    return (users, own_state.reshape(user_state.shape), block, block_state.reshape(item_state.shape))


def solution(mesh):
    return jax.shard_map(
        per_device,
        mesh=mesh,
        in_specs=(
            P(("wide", "narrow"), None),
            P(("wide", "narrow")),
            P("wide", None),
            P("wide"),
            P("wide", "narrow", None, None),
            P("wide", "narrow", None),
            P("wide", "narrow", None, None, None),
            P("wide", "narrow", None, None),
        ),
        out_specs=(P(("wide", "narrow"), None), P(("wide", "narrow")), P("wide", None), P("wide")),
        check_vma=False,
    )
```

```python
import functools

import jax
import jax.numpy as jnp
from jax import lax
from jax.experimental import pallas as pl
from jax.experimental.pallas import tpu as pltpu
from jax.sharding import PartitionSpec as P

TILE = 128
STRATA = 2
BATCH = 4
CHUNKS = 8
AHEAD = 8
LAG_FRESH = 5
LAG_RELAY = 7
WINDOW = TILE + 16
MESH = pl.DeviceIdType.MESH
step_rate = 0.25
f32 = jnp.float32
bf16 = jnp.bfloat16
VMEM = pltpu.MemorySpace.VMEM
SMEM = pltpu.MemorySpace.SMEM


def dot(a, b, dims):
    return lax.dot_general(a, b, (dims, ((), ())), preferred_element_type=f32)


def pair(x):
    high = x.astype(bf16)
    low = (x - high.astype(f32)).astype(bf16)
    return jnp.concatenate([high, low], axis=0)


def tiles_kernel(
    stratum, ids, count, offsets, positives, users, state, block, negatives,
    new_users, new_state, pos_grad, neg_grad, split, square, padded, spread,
):
    cols = block.shape[0] // TILE
    rows = users.shape[0] // TILE
    side = TILE
    width = users.shape[1]
    new_users[...] = jnp.zeros(new_users.shape, f32)
    pos_grad[...] = jnp.zeros(pos_grad.shape, f32)
    spread[...] = jnp.zeros(spread.shape, f32)
    length = negatives.shape[0]
    padded[0:length, :] = negatives[...]
    padded[length:, :] = jnp.zeros((padded.shape[0] - length, width), f32)
    for col in range(cols):
        split[col] = pair(block[col * side : (col + 1) * side, :])
    live_count = count[0, stratum]
    item = lax.broadcasted_iota(jnp.int32, (side, side), 0)
    place = lax.broadcasted_iota(jnp.int32, (side, WINDOW), 1)

    def batch(step, carry):
        work = []
        for lane in range(BATCH):
            slot = step * BATCH + lane
            tile = ids[stratum, slot]
            within = lax.rem(offsets[stratum, slot], 8)
            window = pl.ds(pl.multiple_of(offsets[stratum, slot] - within, 8), WINDOW)
            row = pl.multiple_of(lax.div(tile, cols) * side, side)
            col = lax.rem(tile, cols)
            live = jnp.where(slot < live_count, 1.0 / side, 0.0).astype(f32)
            factors = users[pl.ds(row, side), :]
            factors_low = factors.astype(bf16)
            neg_rows = padded[window, :].astype(bf16)
            hot = jnp.where(item == positives[stratum, pl.ds(slot, 1), :], 1.0, 0.0).astype(f32)
            hot_t = hot.T.astype(bf16)
            hot = hot.astype(bf16)
            pos_rows = dot(jnp.concatenate([hot_t, hot_t], axis=1), split[col], ((1,), (0,)))
            neg_score = dot(factors_low, neg_rows, ((1,), (1,)))
            pos_score = jnp.sum(factors * pos_rows, axis=-1, keepdims=True)
            chosen = jnp.logical_and(place >= within, place < within + side)
            coeffs = jnp.where(chosen, live, 0.0) / (1.0 + jnp.exp(pos_score - neg_score))
            totals = jnp.sum(coeffs, axis=-1, keepdims=True)
            coeffs_low = coeffs.astype(bf16)
            factor_grad = dot(coeffs_low, neg_rows, ((1,), (0,))) - totals * pos_rows
            positive = dot(
                jnp.concatenate([hot, hot], axis=1), pair(totals * factors), ((1,), (0,))
            )
            coeffs_t = coeffs.T.astype(bf16)
            negative = dot(
                jnp.concatenate([coeffs_t, coeffs_t], axis=1), pair(factors), ((1,), (0,))
            )
            work.append((row, col, window, factor_grad, positive, negative))
        for row, col, window, factor_grad, positive, negative in work:
            new_users[pl.ds(row, side), :] += factor_grad
            at = pl.ds(pl.multiple_of(col * side, side), side)
            pos_grad[at, :] -= positive
            spread[window, :] += negative
        return carry

    lax.fori_loop(0, lax.div(live_count + (BATCH - 1), BATCH), batch, 0)
    neg_grad[...] = spread[0:length, :]
    square[...] = jnp.zeros(square.shape, f32)
    square[0:rows, :] = state[...]
    sums = square[...].T
    for row in range(rows):
        at = slice(row * side, (row + 1) * side)
        grad = new_users[at, :]
        fresh = sums[:, row : row + 1] + jnp.sum(grad * grad, axis=-1, keepdims=True) * (1.0 / width)
        new_users[at, :] = users[at, :] - (step_rate / jnp.sqrt(fresh)) * grad
        square[:, row : row + 1] = fresh
    new_state[...] = square[...].T[0:rows, :]


def run_tiles(stratum, ids, count, offsets, positives, users, state, block, negatives):
    width = users.shape[1]
    cols = block.shape[0] // TILE
    return pl.pallas_call(
        functools.partial(tiles_kernel, stratum),
        out_shape=(
            jax.ShapeDtypeStruct(users.shape, f32),
            jax.ShapeDtypeStruct(state.shape, f32),
            jax.ShapeDtypeStruct(block.shape, f32),
            jax.ShapeDtypeStruct(block.shape, f32),
        ),
        in_specs=[pl.BlockSpec(memory_space=SMEM)] * 3 + [pl.BlockSpec(memory_space=VMEM)] * 5,
        out_specs=(pl.BlockSpec(memory_space=VMEM),) * 4,
        scratch_shapes=[
            pltpu.VMEM((cols, 2 * TILE, width), bf16),
            pltpu.VMEM((TILE, TILE), f32),
            pltpu.VMEM((block.shape[0] + 16, width), f32),
            pltpu.VMEM((block.shape[0] + 16, width), f32),
        ],
        compiler_params=pltpu.CompilerParams(vmem_limit_bytes=24 * 1024 * 1024),
        name="tiles",
    )(ids, count, offsets, positives, users, state, block, negatives)


def greet(devices):
    barrier = pltpu.get_barrier_semaphore()
    for device in devices:
        pl.semaphore_signal(barrier, inc=1, device_id=device, device_id_type=MESH)
    pl.semaphore_wait(barrier, len(devices))


def send(src, dst, sems, kind, chunk, device):
    copy = pltpu.make_async_remote_copy(
        src_ref=src,
        dst_ref=dst,
        send_sem=sems.at[0, kind, chunk],
        recv_sem=sems.at[1, kind, chunk],
        device_id=device,
        device_id_type=MESH,
    )
    copy.start()
    return copy


def fetch_kernel(wide, count, *refs):
    block, negatives = refs[0], refs[count]
    sems, local_sems = refs[2 * count + 1 :]
    w, r = lax.axis_index("wide"), lax.axis_index("narrow")
    across = (lax.rem(w + wide // 2, wide), r)
    beside = (w, 1 - r)
    greet([across, beside])
    copies = []
    half = block.shape[0] // 2
    size = half // CHUNKS
    far, near = [], []

    def part(chunk):
        return pl.ds(pl.multiple_of(r * half + chunk * size, size), size)

    for c in range(CHUNKS):
        far.append(send(block.at[part(c), :], negatives.at[part(c), :], sems, 0, c, across))
    for k in range(count):
        copies.append(pltpu.make_async_copy(refs[k], refs[count + 1 + k], local_sems.at[k]))
        copies[k].start()
    for c in range(CHUNKS):
        far[c].wait_recv()
        near.append(send(negatives.at[part(c), :], negatives.at[part(c), :], sems, 1, c, beside))
    for c in range(CHUNKS):
        far[c].wait_send()
        near[c].wait()
    for copy in copies:
        copy.wait()


def run_fetch(*arrays):
    count = len(arrays)
    shapes = [jax.ShapeDtypeStruct(array.shape, array.dtype) for array in (arrays[0],) + arrays]
    return pl.pallas_call(
        functools.partial(fetch_kernel, lax.axis_size("wide"), count),
        out_shape=shapes,
        in_specs=[pl.BlockSpec(memory_space=pltpu.MemorySpace.HBM)] * count,
        out_specs=[pl.BlockSpec(memory_space=VMEM)] * (count + 1),
        scratch_shapes=[
            pltpu.SemaphoreType.DMA((2, 2, CHUNKS)),
            pltpu.SemaphoreType.DMA((count,)),
        ],
        compiler_params=pltpu.CompilerParams(
            collective_id=0, has_side_effects=True, vmem_limit_bytes=8 * 1024 * 1024
        ),
        name="fetch",
    )(*[pltpu.with_memory_space_constraint(a, pltpu.MemorySpace.HBM) for a in arrays])


def exchange_kernel(wide, shifts, last, *refs):
    pos_grad, neg_grad, block, state = refs[:4]
    outs = refs[4 : 4 + len(shifts)]
    new_state = refs[4 + len(shifts)]
    beside_neg, beside_pos, across_neg, summed, fresh_half, fresh_state, square, sems = refs[
        5 + len(shifts) :
    ]
    w, r = lax.axis_index("wide"), lax.axis_index("narrow")
    across = (lax.rem(w + wide // 2, wide), r)
    beside = (w, 1 - r)
    targets = [(lax.rem(w + shift + wide, wide), r) for shift in shifts]
    sources = [(lax.rem(w - shift + wide, wide), r) for shift in shifts]
    greet([beside, across] + targets + sources)
    width = block.shape[1]
    half = block.shape[0] // 2
    size = half // CHUNKS
    side = TILE

    def part(which, chunk):
        return pl.ds(pl.multiple_of(which * half + chunk * size, size), size)

    def local(chunk):
        return slice(chunk * size, (chunk + 1) * size)

    side_neg, side_pos, far, relayed = [], [], [], []
    moved = [[] for shift in shifts]

    def send_neg(c):
        side_neg.append(
            send(neg_grad.at[part(1 - r, c), :], beside_neg.at[local(c), :], sems, 0, c, beside)
        )

    def send_pos(c):
        side_pos.append(
            send(pos_grad.at[part(1 - r, c), :], beside_pos.at[local(c), :], sems, 1, c, beside)
        )

    def send_sum(c):
        side_neg[c].wait_recv()
        summed[local(c), :] = neg_grad[part(r, c), :] + beside_neg[local(c), :]
        far.append(send(summed.at[local(c), :], across_neg.at[local(c), :], sems, 2, c, across))

    def send_fresh(c):
        side_pos[c].wait_recv()
        far[c].wait_recv()
        grad = pos_grad[part(r, c), :] + beside_pos[local(c), :] + across_neg[local(c), :]
        row, begin = c * size // side, c * size % side
        fresh = sums[begin : begin + size, row : row + 1] + jnp.sum(
            grad * grad, axis=-1, keepdims=True
        ) * (1.0 / width)
        fresh_half[local(c), :] = block[part(r, c), :] - (step_rate / jnp.sqrt(fresh)) * grad
        square[begin : begin + size, row : row + 1] = fresh
        for k in reversed(range(len(shifts))):
            moved[k].append(
                send(
                    fresh_half.at[local(c), :], outs[k].at[part(r, c), :], sems, 3 + k, c, targets[k]
                )
            )

    def relay(c):
        for k in range(len(shifts)):
            moved[k][c].wait_recv()
            relayed.append(
                send(outs[k].at[part(r, c), :], outs[k].at[part(r, c), :], sems, 5 + k, c, beside)
            )

    for c in range(AHEAD):
        send_neg(c)
    square[...] = jnp.zeros(square.shape, f32)
    square[0 : half // side, :] = state[r]
    sums = square[...].T
    state_moved = None
    for step in range(CHUNKS + LAG_RELAY):
        if step < CHUNKS:
            send_sum(step)
            if step + AHEAD < CHUNKS:
                send_neg(step + AHEAD)
            send_pos(step)
        if 0 <= step - LAG_FRESH < CHUNKS:
            send_fresh(step - LAG_FRESH)
            if step - LAG_FRESH == CHUNKS - 1:
                fresh_state[...] = square[...].T[0 : half // side, :]
                state_moved = send(fresh_state, new_state.at[r], sems, 7, 0, targets[0])
        if 0 <= step - LAG_RELAY:
            relay(step - LAG_RELAY)
    state_moved.wait_recv()
    if last:
        relayed.append(send(new_state.at[r], new_state.at[r], sems, 7, 1, beside))
    for copies in [side_neg, side_pos, far] + moved + [[state_moved]]:
        for copy in copies:
            copy.wait_send()
    for copy in relayed:
        copy.wait()


def run_exchange(shifts, last, pos_grad, neg_grad, block, state):
    half = (block.shape[0] // 2, block.shape[1])
    outs = (jax.ShapeDtypeStruct(block.shape, f32),) * len(shifts)
    return pl.pallas_call(
        functools.partial(exchange_kernel, lax.axis_size("wide"), shifts, last),
        out_shape=outs + (jax.ShapeDtypeStruct(state.shape, f32),),
        in_specs=[pl.BlockSpec(memory_space=VMEM)] * 4,
        out_specs=(pl.BlockSpec(memory_space=VMEM),) * (len(shifts) + 1),
        scratch_shapes=[pltpu.VMEM(half, f32)] * 5
        + [
            pltpu.VMEM(state.shape[1:], f32),
            pltpu.VMEM((TILE, TILE), f32),
            pltpu.SemaphoreType.DMA((2, 8, CHUNKS)),
        ],
        compiler_params=pltpu.CompilerParams(
            collective_id=2 if last else 1,
            has_side_effects=True,
            vmem_limit_bytes=12 * 1024 * 1024,
        ),
        name="exchange",
    )(pos_grad, neg_grad, block, state)


def passed_along(block, distance):
    size = lax.axis_size("wide")
    return lax.ppermute(block, "wide", [((i - distance) % size, i) for i in range(size)])


def general_exchange(shift, pos_grad, neg_grad, block, state):
    half = lax.axis_size("wide") // 2
    total = lax.psum(pos_grad + passed_along(neg_grad, half), "narrow")
    new_state = state + jnp.mean(total * total, axis=-1)
    block = block - step_rate * total / jnp.sqrt(new_state)[:, None]
    return passed_along((block, new_state), shift)


def per_device(users, user_state, items, item_state, tile_ids, tile_count, pos_items, neg_offsets):
    wide, narrow = lax.axis_size("wide"), lax.axis_size("narrow")
    ids, count = tile_ids[0, 0], tile_count[0]
    positives, offsets = pos_items[0, 0], neg_offsets[0, 0]
    own_state = user_state.reshape(-1, TILE)
    block, block_state = items, item_state
    paired = narrow == 2
    if paired:
        block_state = item_state.reshape(2, -1, TILE)
        negatives, block, users, own_state, positives, block_state, ids, count, offsets = run_fetch(
            block, users, own_state, positives, block_state, ids, count, offsets
        )
    else:
        negatives = passed_along(block, wide // 2)
    for stratum in range(STRATA):
        users, own_state, pos_grad, neg_grad = run_tiles(
            stratum, ids, count, offsets, positives, users, own_state, block, negatives
        )
        last = stratum + 1 == STRATA
        if paired:
            shifts = (1 - STRATA,) if last else (1, 1 + wide // 2)
            results = run_exchange(shifts, last, pos_grad, neg_grad, block, block_state)
            block, block_state = results[0], results[-1]
            negatives = results[1]
        else:
            block, block_state = general_exchange(
                1 - STRATA if last else 1, pos_grad, neg_grad, block, block_state
            )
            if not last:
                negatives = passed_along(block, wide // 2)
    return (users, own_state.reshape(user_state.shape), block, block_state.reshape(item_state.shape))


def solution(mesh):
    return jax.shard_map(
        per_device,
        mesh=mesh,
        in_specs=(
            P(("wide", "narrow"), None),
            P(("wide", "narrow")),
            P("wide", None),
            P("wide"),
            P("wide", "narrow", None, None),
            P("wide", "narrow", None),
            P("wide", "narrow", None, None, None),
            P("wide", "narrow", None, None),
        ),
        out_specs=(P(("wide", "narrow"), None), P(("wide", "narrow")), P("wide", None), P("wide")),
        check_vma=False,
    )
```
